512 devices in a mesh: dp: 8 (over z), frame: 32 (over y_hi, x, core), tile: 2 (over y_lo).
Axes of the slice: x: 4, y: 8 (y_hi: 4, y_lo: 2; y = y_hi * 2 + y_lo), z: 8, core: 2. Of those that a mesh axis runs over, the one named last changes fastest.
Arguments:
- clip_input: bfloat16 [8, 32, 18, 32, 640], P('dp', 'frame', 'tile'), may hold values from -36 to 36
- cotangent: bfloat16 [8, 32, 18, 32, 640], P('dp', 'frame', 'tile'), may hold values from -6 to 6
- norm_gain: float32 [640], replicated, may hold values from 0.25 to 1.75
- conv_weight: bfloat16 [9, 640, 640], P(None, ('frame', 'tile')), may hold values from -0.078125 to 0.078125
- attn_weight: bfloat16 [640, 2560], P(('frame', 'tile')), may hold values from -0.25 to 0.25
- query_gain: float32 [64], replicated, may hold values from 0.5 to 1.5
- key_gain: float32 [64], replicated, may hold values from 0.5 to 1.5
- logit_scale: float32 [10], replicated, may hold values from 0.5 to 4
Outputs:
- mid_grad: bfloat16 [8, 32, 18, 32, 640], P('dp', 'frame', 'tile')
- value_grad: float32 [640, 640], P(('frame', 'tile'))
- out_proj_grad: float32 [640, 640], P(('frame', 'tile'))
- query_gain_grad: float32 [64], replicated
- key_gain_grad: float32 [64], replicated
- scale_grad: float32 [10], replicated
The draws below stay inside these ranges and needn't reach their ends.
All inputs are finite; a program needn't handle non-finite values.
Results may differ from the reference program's by a relative error of at most 0.013.
The reference program's roundings to bfloat16 on the way count: a program that leaves them out, or rounds other values in their place, can miss the bound.
Values may be sent and summed in bfloat16 or wider, within the bound.
A program may use at most 128 MiB of HBM per device.

```python
import math
import jax
import jax.numpy as jnp
from jax import lax

C = 640
HEADS = 10
DH = 64
GROUPS = 32
H = 18
W = 32
FRAMES = 32
CLIPS = 8
TOKENS = 147456


def draw_clip_input(key, part):
    key_base, key_rows, key_chan = jax.random.split(jax.random.fold_in(key, 7), 3)
    shape = (CLIPS, FRAMES, H, W, C)
    base = jnp.clip(jax.random.normal(key_base, shape, jnp.float32), -4.0, 4.0)
    rise = jnp.exp(math.log(3.0) * jnp.arange(H, dtype=jnp.float32) / max(H - 1, 1))
    rough = jnp.exp(math.log(10.0) * jax.random.uniform(key_rows, (CLIPS, FRAMES, H, 1, 1), jnp.float32))
    chan = jnp.exp(jax.random.uniform(key_chan, (C,), jnp.float32, math.log(0.3), math.log(3.0)))
    return (base * 0.1 * rise[None, None, :, None, None] * rough * chan).astype(jnp.bfloat16)


def steps_of(key, extent, shards, least, high):
    loudness, own = 1.0, jax.random.fold_in(key, 6)
    for dim, blocks in shards:
        draws = jnp.exp(jax.random.uniform(jax.random.fold_in(own, dim), (blocks,), jnp.float32, least / len(shards), high / len(shards)))
        loudness = loudness * jnp.repeat(draws, extent[dim] // blocks).reshape([-1 if axis == dim else 1 for axis in range(len(extent))])
    return loudness


def centred(rng, dims, scale, limit, cuts=(), held_as=jnp.bfloat16):
    array = jax.random.normal(rng, dims, jnp.float32) * scale
    if len(cuts) > 0:
        array = steps_of(rng, dims, cuts, -0.22, 0.18) * array
    return jnp.clip(array, min=-limit, max=limit).astype(held_as)


def setup_inputs(seed: int = 0) -> dict:
    streams_of = jax.random.split(jax.random.key(seed), 9)
    clip_input = draw_clip_input(jax.random.fold_in(streams_of[8], 71), 0)
    cotangent = centred(streams_of[1], (CLIPS, FRAMES, H, W, C), 1.0, 6.0, ((0, 8), (1, 32), (2, 2)))
    norm_gain = jnp.clip(1.0 + 0.15 * jax.random.normal(streams_of[2], (C,), jnp.float32), 0.25, 1.75)
    conv_weight = centred(streams_of[3], (9, C, C), (9 * C) ** -0.5, 0.078125, ((1, 64),))
    attn_weight = centred(streams_of[4], (C, 4 * C), C ** -0.5, 0.25, ((0, 64),))
    query_gain = jnp.clip(1.0 + 0.1 * jax.random.normal(streams_of[5], (DH,), jnp.float32), 0.5, 1.5)
    key_gain = jnp.clip(1.0 + 0.1 * jax.random.normal(streams_of[6], (DH,), jnp.float32), 0.5, 1.5)
    logit_scale = jnp.clip(jnp.exp(jax.random.uniform(streams_of[7], (HEADS,), jnp.float32, math.log(0.5), math.log(4.0))), 0.5, 4.0)
    return dict(clip_input=clip_input, cotangent=cotangent, norm_gain=norm_gain, conv_weight=conv_weight, attn_weight=attn_weight, query_gain=query_gain, key_gain=key_gain, logit_scale=logit_scale)


def layer_stats(vec):
    mean = lax.optimization_barrier(jnp.mean(vec, axis=-1, keepdims=True))
    cent = vec - mean
    var = lax.optimization_barrier(jnp.mean(cent * cent, axis=-1, keepdims=True))
    rstd = lax.rsqrt(var + 1e-05)
    return (cent * rstd, rstd)

def layer_back(dhat, hat, rstd):
    first = lax.optimization_barrier(jnp.mean(dhat, axis=-1, keepdims=True))
    second = lax.optimization_barrier(jnp.mean(dhat * hat, axis=-1, keepdims=True))
    return rstd * (dhat - first - hat * second)

def attention_pass(mid, cot, weights, query_gain, key_gain, logit_scale):
    frames, count, width = mid.shape
    heads = logit_scale.shape[0]
    depth = width // heads
    total = frames * count
    high = lax.Precision.HIGHEST
    flat = mid.reshape(total, width)
    proj = jnp.dot(flat, weights[:, :3 * width], preferred_element_type=jnp.float32)
    query = proj[:, :width].reshape(frames, count, heads, depth)
    keyed = proj[:, width:2 * width].reshape(frames, count, heads, depth)
    value = proj[:, 2 * width:].astype(jnp.bfloat16).reshape(frames, count, heads, depth)
    q_hat, q_rstd = layer_stats(query)
    k_hat, k_rstd = layer_stats(keyed)
    q_norm = q_hat * query_gain
    k_norm = k_hat * key_gain
    root = math.sqrt(depth)
    raw = jnp.einsum('fnhd,gnhd->nhfg', q_norm, k_norm, precision=high) / root
    scale = logit_scale[None, :, None, None]
    expo = jnp.exp(raw * scale)
    probs = expo / lax.optimization_barrier(jnp.sum(expo, axis=-1, keepdims=True))
    probs_b = probs.astype(jnp.bfloat16)
    mixed = jnp.einsum('nhfg,gnhd->fnhd', probs_b.astype(jnp.float32), value.astype(jnp.float32), precision=high)
    mixed = mixed.astype(jnp.bfloat16).reshape(total, width)
    cot_flat = cot.reshape(total, width)
    w_out = weights[:, 3 * width:]
    d_mixed = jnp.dot(cot_flat, w_out.T, preferred_element_type=jnp.float32)
    d_mixed = d_mixed.astype(jnp.bfloat16).reshape(frames, count, heads, depth)
    d_probs = jnp.einsum('fnhd,gnhd->nhfg', d_mixed.astype(jnp.float32), value.astype(jnp.float32), precision=high)
    d_value = jnp.einsum('nhfg,fnhd->gnhd', probs_b.astype(jnp.float32), d_mixed.astype(jnp.float32), precision=high)
    d_value = d_value.astype(jnp.bfloat16)
    d_logits = probs * (d_probs - lax.optimization_barrier(jnp.sum(probs * d_probs, axis=-1, keepdims=True)))
    scale_term = lax.optimization_barrier(jnp.sum(d_logits * raw, axis=(0, 2, 3)))
    d_raw = d_logits * scale / root
    d_qn = jnp.einsum('nhfg,gnhd->fnhd', d_raw, k_norm, precision=high)
    d_kn = jnp.einsum('nhfg,fnhd->gnhd', d_raw, q_norm, precision=high)
    qgain_term = lax.optimization_barrier(jnp.sum(d_qn * q_hat, axis=(0, 1, 2)))
    kgain_term = lax.optimization_barrier(jnp.sum(d_kn * k_hat, axis=(0, 1, 2)))
    d_query = layer_back(d_qn * query_gain, q_hat, q_rstd).astype(jnp.bfloat16)
    d_key = layer_back(d_kn * key_gain, k_hat, k_rstd).astype(jnp.bfloat16)
    d_cat = jnp.concatenate([d_query.reshape(total, width), d_key.reshape(total, width), d_value.reshape(total, width)], axis=1)
    d_mid = jnp.dot(d_cat, weights[:, :3 * width].T, preferred_element_type=jnp.float32)
    d_mid = d_mid.astype(jnp.bfloat16).reshape(frames, count, width)
    return (d_mid, mixed, d_value.reshape(total, width), scale_term, qgain_term, kgain_term)

def reference(clip_input, cotangent, norm_gain, conv_weight, attn_weight, query_gain, key_gain, logit_scale):
    width = C
    per_group = width // GROUPS

    def one_clip(pair):
        source, cot = pair
        frames = source.shape[0]
        xf = source.astype(jnp.float32).reshape(frames, H * W, GROUPS, per_group)
        count = H * W * per_group
        mean = lax.optimization_barrier(jnp.sum(xf, axis=(1, 3))) / count
        meansq = lax.optimization_barrier(jnp.sum(xf * xf, axis=(1, 3))) / count
        rstd = lax.rsqrt(meansq - mean * mean + 1e-05)
        normed = (xf - mean[:, None, :, None]) * rstd[:, None, :, None]
        zed = normed.reshape(frames, H, W, width) * norm_gain
        act = jax.nn.silu(zed).astype(jnp.bfloat16)
        padded = jnp.pad(act, ((0, 0), (1, 1), (1, 1), (0, 0)))
        slabs = []
        for row_off in (-1, 0, 1):
            for col_off in (-1, 0, 1):
                slabs.append(padded[:, 1 + row_off:1 + row_off + H, 1 + col_off:1 + col_off + W, :])
        stacked = jnp.concatenate(slabs, axis=-1).reshape(frames * H * W, 9 * width)
        pre = jnp.dot(stacked, conv_weight.reshape(9 * width, width), preferred_element_type=jnp.float32)
        mid = (source.astype(jnp.float32) + pre.reshape(frames, H, W, width)).astype(jnp.bfloat16)
        mid_rows = mid.reshape(frames, H * W, width)
        cot_rows = cot.reshape(frames, H * W, width)
        d_mid, mixed, d_value, scale_term, qgain_term, kgain_term = attention_pass(mid_rows, cot_rows, attn_weight, query_gain, key_gain, logit_scale)
        grad_here = (cot.astype(jnp.float32) + d_mid.reshape(frames, H, W, width).astype(jnp.float32)).astype(jnp.bfloat16)
        flat_mid = mid_rows.reshape(frames * H * W, width)
        flat_cot = cot_rows.reshape(frames * H * W, width)
        vgrad = jnp.dot(flat_mid.T, d_value, preferred_element_type=jnp.float32)
        ograd = jnp.dot(mixed.T, flat_cot, preferred_element_type=jnp.float32)
        return (grad_here, vgrad, ograd, scale_term, qgain_term, kgain_term)
    outs = lax.map(one_clip, (clip_input, cotangent))
    factor = 1.0 / math.sqrt(TOKENS)
    mid_grad = outs[0]
    value_grad = lax.optimization_barrier(jnp.sum(outs[1], axis=0)) * factor
    out_proj_grad = lax.optimization_barrier(jnp.sum(outs[2], axis=0)) * factor
    scale_grad = lax.optimization_barrier(jnp.sum(outs[3], axis=0)) * factor
    query_gain_grad = lax.optimization_barrier(jnp.sum(outs[4], axis=0)) * factor
    key_gain_grad = lax.optimization_barrier(jnp.sum(outs[5], axis=0)) * factor
    return (mid_grad, value_grad, out_proj_grad, query_gain_grad, key_gain_grad, scale_grad)
```

```python
import math

import jax
import jax.numpy as jnp
from jax import lax
from jax.experimental import pallas as pl
from jax.experimental.pallas import tpu as pltpu
from jax.sharding import PartitionSpec as P

GROUPS = 32


def gather_kernel(w_ref, out_ref, send_sem, recv_sem, own_sem):
    frame, yl = (lax.axis_index("frame"), lax.axis_index("tile"))
    core = frame % 2
    x = (frame // 2) % 4
    y = (frame // 8) * 2 + yl

    def place(dy, dx, dc):
        yy, xx, cc = ((y + dy + 8) % 8, (x + dx + 4) % 4, (core + dc) % 2)
        return ((yy // 2) * 8 + xx * 2 + cc, yy % 2)

    def slot(dy, dx, dc):
        ff, tt = place(dy, dx, dc)
        return ff * 2 + tt

    sent = []

    def send(block, to, own=False):
        ff, tt = place(*to)
        at = slot(*block)
        copy = pltpu.make_async_remote_copy(
            src_ref=w_ref if own else out_ref.at[at],
            dst_ref=out_ref.at[at],
            send_sem=send_sem.at[len(sent)],
            recv_sem=recv_sem.at[at],
            device_id={"frame": ff, "tile": tt},
            device_id_type=pl.DeviceIdType.MESH,
        )
        copy.start()
        sent.append(copy)

    def arrived(block):
        at = slot(*block)
        pltpu.make_async_remote_copy(
            src_ref=out_ref.at[at],
            dst_ref=out_ref.at[at],
            send_sem=send_sem.at[0],
            recv_sem=recv_sem.at[at],
            device_id={"frame": frame, "tile": yl},
            device_id_type=pl.DeviceIdType.MESH,
        ).wait_recv()

    up, down, right, left, twin = ((1, 0, 0), (-1, 0, 0), (0, 1, 0), (0, -1, 0), (0, 0, 1))
    barrier = pltpu.get_barrier_semaphore()
    for to in (up, down, right, left, twin):
        ff, tt = place(*to)
        pl.semaphore_signal(
            barrier,
            inc=1,
            device_id={"frame": ff, "tile": tt},
            device_id_type=pl.DeviceIdType.MESH,
        )
    pl.semaphore_wait(barrier, 5)
    mine = pltpu.make_async_copy(w_ref, out_ref.at[slot(0, 0, 0)], own_sem)
    mine.start()
    for to in (right, left, up, down, twin):
        send((0, 0, 0), to, own=True)
    order = [0, -1, 1, -2, 2, -3, 3, -4]
    for dy in order[1:]:
        arrived((dy, 0, 0))
        if dy < 0 and dy > -4:
            send((dy, 0, 0), up)
        if dy > 0 and dy < 3:
            send((dy, 0, 0), down)
        for to in (right, left, twin):
            send((dy, 0, 0), to)
    for k, dy in enumerate(order):
        arrived((dy, -1, 0))
        if k % 2 == 0:
            send((dy, -1, 0), right)
        send((dy, -1, 0), twin)
        arrived((dy, 1, 0))
        if k % 2 == 1:
            send((dy, 1, 0), left)
        send((dy, 1, 0), twin)
    for dy in order:
        arrived((dy, 2, 0))
        send((dy, 2, 0), twin)
    for dy in order:
        for dx in (0, -1, 1, 2):
            arrived((dy, dx, 1))
    mine.wait()
    for copy in sent:
        copy.wait_send()


def gathered(shard):
    return pl.pallas_call(
        gather_kernel,
        out_shape=jax.ShapeDtypeStruct((64,) + shard.shape, shard.dtype),
        in_specs=[pl.BlockSpec(memory_space=pltpu.VMEM)],
        out_specs=pl.BlockSpec(memory_space=pl.ANY),
        scratch_shapes=[
            pltpu.SemaphoreType.DMA((63,)),
            pltpu.SemaphoreType.DMA((64,)),
            pltpu.SemaphoreType.DMA,
        ],
        compiler_params=pltpu.CompilerParams(collective_id=0, has_side_effects=True),
    )(shard)


def layer_stats(vec):
    mean = jnp.mean(vec, axis=-1, keepdims=True)
    cent = vec - mean
    var = jnp.mean(cent * cent, axis=-1, keepdims=True)
    rstd = lax.rsqrt(var + 1e-05)
    return (cent * rstd, rstd)


def layer_back(dhat, hat, rstd):
    first = jnp.mean(dhat, axis=-1, keepdims=True)
    second = jnp.mean(dhat * hat, axis=-1, keepdims=True)
    return rstd * (dhat - first - hat * second)


def attention_pass(mid, cot, weights, query_gain, key_gain, logit_scale):
    frames, count, width = mid.shape
    heads = logit_scale.shape[0]
    depth = width // heads
    total = frames * count
    high = lax.Precision.HIGHEST
    f32 = jnp.float32
    flat = mid.reshape(total, width)
    w_inner = jnp.concatenate([weights[0], weights[1], weights[2]], axis=1)
    proj = jnp.dot(flat, w_inner, preferred_element_type=f32)
    query = proj[:, :width].reshape(frames, count, heads, depth)
    keyed = proj[:, width : 2 * width].reshape(frames, count, heads, depth)
    value = proj[:, 2 * width :].astype(jnp.bfloat16).reshape(frames, count, heads, depth)
    q_hat, q_rstd = layer_stats(query)
    k_hat, k_rstd = layer_stats(keyed)
    q_norm = q_hat * query_gain
    k_norm = k_hat * key_gain
    root = math.sqrt(depth)
    raw = jnp.einsum("fnhd,gnhd->nhfg", q_norm, k_norm, precision=high) / root
    scale = logit_scale[None, :, None, None]
    expo = jnp.exp(raw * scale)
    probs = expo / jnp.sum(expo, axis=-1, keepdims=True)
    probs_b = probs.astype(jnp.bfloat16)
    mixed = jnp.einsum("nhfg,gnhd->fnhd", probs_b, value, preferred_element_type=f32)
    mixed = mixed.astype(jnp.bfloat16).reshape(total, width)
    cot_flat = cot.reshape(total, width)
    w_out = weights[3]
    d_mixed = lax.dot_general(cot_flat, w_out, (((1,), (1,)), ((), ())), preferred_element_type=f32)
    d_mixed = d_mixed.astype(jnp.bfloat16).reshape(frames, count, heads, depth)
    d_probs = jnp.einsum("fnhd,gnhd->nhfg", d_mixed, value, preferred_element_type=f32)
    d_value = jnp.einsum("nhfg,fnhd->gnhd", probs_b, d_mixed, preferred_element_type=f32)
    d_value = d_value.astype(jnp.bfloat16)
    d_logits = probs * (d_probs - jnp.sum(probs * d_probs, axis=-1, keepdims=True))
    scale_term = jnp.sum(d_logits * raw, axis=(0, 2, 3))
    d_raw = d_logits * scale / root
    d_qn = jnp.einsum("nhfg,gnhd->fnhd", d_raw, k_norm, precision=high)
    d_kn = jnp.einsum("nhfg,fnhd->gnhd", d_raw, q_norm, precision=high)
    qgain_term = jnp.sum(d_qn * q_hat, axis=(0, 1, 2))
    kgain_term = jnp.sum(d_kn * k_hat, axis=(0, 1, 2))
    d_query = layer_back(d_qn * query_gain, q_hat, q_rstd).astype(jnp.bfloat16)
    d_key = layer_back(d_kn * key_gain, k_hat, k_rstd).astype(jnp.bfloat16)
    d_cat = jnp.concatenate(
        [d_query.reshape(total, width), d_key.reshape(total, width), d_value.reshape(total, width)],
        axis=1,
    )
    d_mid = lax.dot_general(d_cat, w_inner, (((1,), (1,)), ((), ())), preferred_element_type=f32)
    d_mid = d_mid.astype(jnp.bfloat16).reshape(frames, count, width)
    return (d_mid, mixed, d_value.reshape(total, width), scale_term, qgain_term, kgain_term)


def exchanged(blocks, small, axes):
    count, rows, width = blocks.shape
    length = small.shape[0]
    high = lax.reduce_precision(small, 8, 7)
    row = jnp.concatenate([high, small - high]).astype(jnp.bfloat16)
    row = jnp.pad(row, (0, width - 2 * length))
    both = jnp.concatenate([blocks, jnp.broadcast_to(row, (count, 1, width))], axis=1)
    got = lax.all_to_all(both, axes, split_axis=0, concat_axis=0, tiled=True)
    total = jnp.sum(got.astype(jnp.float32), axis=0)
    last = total[rows]
    return (total[:rows], last[:length] + last[length : 2 * length])


def local(
    clip_input, cotangent, norm_gain, conv_weight, attn_weight, query_gain, key_gain, logit_scale
):
    source = clip_input[0]
    cot = cotangent[0]
    frames_here, rows, cols, width = source.shape
    positions = rows * cols
    per_group = width // GROUPS
    cot_flat = cot.reshape(frames_here, positions, width)
    shard = jnp.concatenate(
        [
            conv_weight.reshape(90, width),
            jnp.transpose(attn_weight.reshape(10, 4, width), (1, 0, 2)).reshape(40, width),
        ],
        axis=0,
    )
    full = gathered(shard).reshape(64, 13, 10, width).transpose(1, 0, 2, 3)
    full = full.reshape(13, width, width)
    full_conv, attn_full = (full[:9], full[9:])
    tile = lax.axis_index("tile")
    swap = [(0, 1), (1, 0)]
    edge = jnp.where(tile == 0, source[:, rows - 1 :], source[:, :1])
    other_edge = lax.ppermute(edge, "tile", swap)
    xf = source.astype(jnp.float32).reshape(frames_here, positions, GROUPS, per_group)
    part = jnp.concatenate([jnp.sum(xf, axis=(1, 3)), jnp.sum(xf * xf, axis=(1, 3))], axis=1)
    part = part + lax.ppermute(part, "tile", swap)
    sums, squares = (part[:, :GROUPS], part[:, GROUPS:])
    count = positions * lax.axis_size("tile") * per_group
    mean = sums / count
    rstd = lax.rsqrt(squares / count - mean * mean + 1e-05)
    mean_wide = jnp.repeat(mean, per_group, axis=1)[:, None, None, :]
    rstd_wide = jnp.repeat(rstd, per_group, axis=1)[:, None, None, :]

    def activated(v):
        normed = (v.astype(jnp.float32) - mean_wide) * rstd_wide
        return jax.nn.silu(normed * norm_gain).astype(jnp.bfloat16)

    act = activated(source)
    halo = activated(other_edge)
    none = jnp.zeros_like(halo)
    before = jnp.where(tile == 1, halo, none)
    after = jnp.where(tile == 0, halo, none)
    padded = jnp.concatenate([before, act, after], axis=1)
    padded = jnp.pad(padded, ((0, 0), (0, 0), (1, 1), (0, 0)))
    slabs = []
    for row_off in (-1, 0, 1):
        for col_off in (-1, 0, 1):
            slabs.append(
                padded[:, 1 + row_off : 1 + row_off + rows, 1 + col_off : 1 + col_off + cols, :]
            )
    stacked = jnp.stack(slabs, axis=3).reshape(frames_here * positions, 9, width)
    pre = jnp.dot(
        stacked.reshape(frames_here * positions, 9 * width),
        full_conv.reshape(9 * width, width),
        preferred_element_type=jnp.float32,
    )
    mid = (source.astype(jnp.float32) + pre.reshape(frames_here, rows, cols, width)).astype(
        jnp.bfloat16
    )
    mid_flat = mid.reshape(frames_here, positions, width)
    mid_tiled, cot_tiled = (
        lax.all_to_all(mid_flat, "frame", split_axis=1, concat_axis=0, tiled=True),
        lax.all_to_all(cot_flat, "frame", split_axis=1, concat_axis=0, tiled=True),
    )
    d_mid, mixed, d_value, scale_term, qgain_term, kgain_term = attention_pass(
        mid_tiled, cot_tiled, attn_full, query_gain, key_gain, logit_scale
    )
    d_back = lax.all_to_all(d_mid, "frame", split_axis=0, concat_axis=1, tiled=True)
    mid_grad = (
        cot.astype(jnp.float32) + d_back.reshape(frames_here, rows, cols, width).astype(jnp.float32)
    ).astype(jnp.bfloat16)
    tiled_mid = mid_tiled.reshape(-1, width)
    tiled_cot = cot_tiled.reshape(-1, width)
    contract = (((0,), (0,)), ((), ()))
    value_term = lax.dot_general(tiled_mid, d_value, contract, preferred_element_type=jnp.float32)
    out_term = lax.dot_general(mixed, tiled_cot, contract, preferred_element_type=jnp.float32)
    terms = jnp.concatenate([value_term, out_term], axis=1).astype(jnp.bfloat16)
    small = jnp.concatenate([scale_term, qgain_term, kgain_term])
    heads, depth = (logit_scale.shape[0], query_gain.shape[0])
    plane = exchanged(terms.reshape(64, 10, 2 * width), small, ("frame", "tile"))
    block = plane[0].astype(jnp.bfloat16)
    summed, small = exchanged(jnp.broadcast_to(block, (8, 10, 2 * width)), plane[1], "dp")
    scale_sum = small[:heads]
    qgain_sum = small[heads : heads + depth]
    kgain_sum = small[heads + depth :]
    tokens_all = lax.axis_size("dp") * mid_tiled.shape[0] * rows * lax.axis_size("tile") * cols
    factor = 1.0 / math.sqrt(tokens_all)
    value_grad = summed[:, :width] * factor
    out_proj_grad = summed[:, width:] * factor
    return (
        mid_grad[None],
        value_grad,
        out_proj_grad,
        qgain_sum * factor,
        kgain_sum * factor,
        scale_sum * factor,
    )


def solution(mesh):
    in_specs = (
        P("dp", "frame", "tile", None, None),
        P("dp", "frame", "tile", None, None),
        P(),
        P(None, ("frame", "tile"), None),
        P(("frame", "tile"), None),
        P(),
        P(),
        P(),
    )
    out_specs = (
        P("dp", "frame", "tile", None, None),
        P(("frame", "tile"), None),
        P(("frame", "tile"), None),
        P(),
        P(),
        P(),
    )
    return jax.shard_map(local, mesh=mesh, in_specs=in_specs, out_specs=out_specs, check_vma=False)
```

```python
import math

import jax
import jax.numpy as jnp
from jax import lax
from jax.experimental import pallas as pl
from jax.experimental.pallas import tpu as pltpu
from jax.sharding import PartitionSpec as P

GROUPS = 32


MESH = pl.DeviceIdType.MESH


def spot():
    frame, yl = (lax.axis_index("frame"), lax.axis_index("tile"))
    return ((frame // 8) * 2 + yl, (frame // 2) % 4, frame % 2)


def named(y, x, core):
    return {"frame": (y // 2) * 8 + x * 2 + core, "tile": y % 2}


def greet(peers):
    barrier = pltpu.get_barrier_semaphore()
    for peer in peers:
        pl.semaphore_signal(barrier, inc=1, device_id=peer, device_id_type=MESH)
    pl.semaphore_wait(barrier, len(peers))


def column_kernel(w_ref, out_ref, send_sem, recv_sem, own_sem):
    y, x, core = spot()
    up, down = (named((y + 1) % 8, x, core), named((y + 7) % 8, x, core))
    greet((up, down))
    sent = []

    def remote(at, to, number, own=False):
        return pltpu.make_async_remote_copy(
            src_ref=w_ref if own else out_ref.at[at],
            dst_ref=out_ref.at[at],
            send_sem=send_sem.at[number],
            recv_sem=recv_sem.at[at],
            device_id=to,
            device_id_type=MESH,
        )

    def send(dy, to, own=False):
        copy = remote((y + dy + 8) % 8, to, len(sent), own)
        copy.start()
        sent.append(copy)

    def arrived(dy):
        remote((y + dy + 8) % 8, up, 0).wait_recv()

    send(0, up, True)
    send(0, down, True)
    mine = pltpu.make_async_copy(w_ref, out_ref.at[y], own_sem)
    mine.start()
    for step in (1, 2, 3):
        arrived(-step)
        send(-step, up)
        arrived(step)
        if step < 3:
            send(step, down)
    arrived(-4)
    mine.wait()
    for copy in sent:
        copy.wait_send()


def wide_kernel(conv_in, attn_in, conv_out, attn_out, send_sem, recv_sem, whole_sem, own_sem):
    y, x, core = spot()
    z = lax.axis_index("dp")
    parity = z % 2
    ahead, behind = ({"dp": (z + 1) % 8}, {"dp": (z + 7) % 8})
    right, left = (named(y, (x + 1) % 4, core), named(y, (x + 3) % 4, core))
    twin = named(y, x, 1 - core)
    greet((ahead, behind, right, left, twin))
    sent = []

    def rows(dx, dc=0):
        number = ((x + dx + 4) % 4) * 2 + (core + dc) % 2
        return (number, pl.ds(pl.multiple_of(number * 80, 16), 80))

    def parts(unit):
        attn, at = unit
        if attn:
            return (attn_in, attn_out, at, 9 + at)
        return (conv_in, conv_out, at, at)

    def remote(unit, dx, dc, to, number, own=False):
        source, target, at, sem = parts(unit)
        block, span = rows(dx, dc)
        there = target.at[at, span]
        return pltpu.make_async_remote_copy(
            src_ref=source.at[at] if own else there,
            dst_ref=there,
            send_sem=send_sem.at[number],
            recv_sem=recv_sem.at[sem, block],
            device_id=to,
            device_id_type=MESH,
        )

    def send(unit, dx, to, own=False):
        copy = remote(unit, dx, 0, to, len(sent), own)
        copy.start()
        sent.append(copy)

    def arrived(unit, dx, dc=0):
        remote(unit, dx, dc, twin, 0).wait_recv()

    near = [(False, 2 * j + parity) for j in range(4)] + [(True, 2 * j + parity) for j in range(2)]
    far = [(False, 2 * j + 1 - parity) for j in range(4)]
    far = far + [(True, 2 * j + 1 - parity) for j in range(2)]
    near = near + [(False, 8)]
    for unit in near:
        send(unit, 0, right, True)
        send(unit, 0, left, True)
    span = rows(0)[1]
    pairs = ((conv_in, conv_out, 0), (attn_in, attn_out, 1))
    wholes = []
    for source, target, k in pairs:
        copy = pltpu.make_async_remote_copy(
            src_ref=source,
            dst_ref=target.at[:, span],
            send_sem=whole_sem.at[k],
            recv_sem=whole_sem.at[2 + k],
            device_id=twin,
            device_id_type=MESH,
        )
        copy.start()
        wholes.append(copy)
    locals_ = []
    for source, target, k in pairs:
        copy = pltpu.make_async_copy(source, target.at[:, span], own_sem.at[k])
        copy.start()
        locals_.append(copy)

    def onward(k, dx):
        if k < 6:
            send(near[k], dx, ahead if k % 2 == 0 else behind)
        send(near[k], dx, twin)

    def across(k, dx):
        arrived(far[k], dx)
        send(far[k], dx, twin)

    for k, unit in enumerate(near):
        arrived(unit, -1)
        if k % 2 == 0:
            send(unit, -1, right)
        onward(k, -1)
        arrived(unit, 1)
        if k % 2 == 1:
            send(unit, 1, left)
        onward(k, 1)
        if k >= 1:
            across(k - 1, -1)
            across(k - 1, 1)
    for k, unit in enumerate(near):
        arrived(unit, 2)
        onward(k, 2)
        if k >= 1:
            across(k - 1, 2)
    for copy in wholes:
        copy.wait_recv()
    for unit in near + far:
        for dx in (-1, 1, 2):
            arrived(unit, dx, 1)
    for copy in locals_:
        copy.wait()
    for copy in wholes + sent:
        copy.wait_send()


def column(shard):
    return pl.pallas_call(
        column_kernel,
        out_shape=jax.ShapeDtypeStruct((8,) + shard.shape, shard.dtype),
        in_specs=[pl.BlockSpec(memory_space=pltpu.VMEM)],
        out_specs=pl.BlockSpec(memory_space=pl.ANY),
        scratch_shapes=[
            pltpu.SemaphoreType.DMA((7,)),
            pltpu.SemaphoreType.DMA((8,)),
            pltpu.SemaphoreType.DMA,
        ],
        compiler_params=pltpu.CompilerParams(collective_id=0, has_side_effects=True),
    )(shard)


def widened(conv, attn):
    width = conv.shape[2]
    return pl.pallas_call(
        wide_kernel,
        out_shape=(
            jax.ShapeDtypeStruct((9, width, width), conv.dtype),
            jax.ShapeDtypeStruct((4, width, width), attn.dtype),
        ),
        in_specs=[pl.BlockSpec(memory_space=pltpu.VMEM)] * 2,
        out_specs=(pl.BlockSpec(memory_space=pl.ANY),) * 2,
        scratch_shapes=[
            pltpu.SemaphoreType.DMA((78,)),
            pltpu.SemaphoreType.DMA((13, 8)),
            pltpu.SemaphoreType.DMA((4,)),
            pltpu.SemaphoreType.DMA((2,)),
        ],
        compiler_params=pltpu.CompilerParams(collective_id=1, has_side_effects=True),
    )(conv, attn)


def clips_kernel(in_ref, out_ref, held, send_sem, recv_sem, own_sem):
    z = lax.axis_index("dp")
    greet([{"dp": (z + d) % 8} for d in range(1, 8)])
    mine = pltpu.make_async_copy(in_ref, held.at[z], own_sem)
    mine.start()
    copies = []
    for d in (4, 3, 5, 2, 6, 1, 7):
        copy = pltpu.make_async_remote_copy(
            src_ref=in_ref,
            dst_ref=held.at[z],
            send_sem=send_sem.at[d],
            recv_sem=recv_sem.at[z],
            device_id={"dp": (z + d) % 8},
            device_id_type=MESH,
        )
        copy.start()
        copies.append(copy)
    for d in range(1, 8):
        peer = (z + d) % 8
        pltpu.make_async_remote_copy(
            src_ref=in_ref,
            dst_ref=held.at[peer],
            send_sem=send_sem.at[0],
            recv_sem=recv_sem.at[peer],
            device_id={"dp": peer},
            device_id_type=MESH,
        ).wait_recv()
    mine.wait()
    total = held[0].astype(jnp.float32)
    for k in range(1, 8):
        total = total + held[k].astype(jnp.float32)
    out_ref[...] = total
    for copy in copies:
        copy.wait_send()


def over_clips(block):
    return pl.pallas_call(
        clips_kernel,
        out_shape=jax.ShapeDtypeStruct(block.shape, jnp.float32),
        in_specs=[pl.BlockSpec(memory_space=pltpu.VMEM)],
        out_specs=pl.BlockSpec(memory_space=pltpu.VMEM),
        scratch_shapes=[
            pltpu.VMEM((8,) + block.shape, block.dtype),
            pltpu.SemaphoreType.DMA((8,)),
            pltpu.SemaphoreType.DMA((8,)),
            pltpu.SemaphoreType.DMA,
        ],
        compiler_params=pltpu.CompilerParams(collective_id=2, has_side_effects=True),
    )(block)


def reorder(width):
    place = lax.broadcasted_iota(jnp.int32, (width, width), 1)
    origin = ((place // 20) % 4) * 160 + (place // 80) * 20 + place % 20
    return (lax.broadcasted_iota(jnp.int32, (width, width), 0) == origin).astype(jnp.bfloat16)


def paired(term):
    width = term.shape[1]
    tile = lax.axis_index("tile")
    halves = term.reshape(32, 2, 10, width)
    mine = lax.dynamic_index_in_dim(halves, tile, 1, keepdims=False)
    theirs = lax.dynamic_index_in_dim(halves, 1 - tile, 1, keepdims=False).astype(jnp.bfloat16)
    got = lax.ppermute(theirs, "tile", [(0, 1), (1, 0)])
    return (mine + got.astype(jnp.float32)).astype(jnp.bfloat16)


def over_frames(blocks):
    got = lax.all_to_all(blocks, "frame", split_axis=0, concat_axis=0, tiled=True)
    return jnp.sum(got.astype(jnp.float32), axis=0)


def two_parts(small, width):
    high = lax.reduce_precision(small, 8, 7)
    row = jnp.concatenate([high, small - high]).astype(jnp.bfloat16)
    return jnp.pad(row, (0, width - row.shape[0]))[None]


def one_part(row, length):
    return row[:length] + row[length : 2 * length]


def layer_stats(vec):
    mean = jnp.mean(vec, axis=-1, keepdims=True)
    cent = vec - mean
    var = jnp.mean(cent * cent, axis=-1, keepdims=True)
    rstd = lax.rsqrt(var + 1e-05)
    return (cent * rstd, rstd)


def layer_back(dhat, hat, rstd):
    first = jnp.mean(dhat, axis=-1, keepdims=True)
    second = jnp.mean(dhat * hat, axis=-1, keepdims=True)
    return rstd * (dhat - first - hat * second)


def attention_pass(mid, cot, weights, order, query_gain, key_gain, logit_scale):
    frames, count, width = mid.shape
    heads = logit_scale.shape[0]
    depth = width // heads
    total = frames * count
    high = lax.Precision.HIGHEST
    f32 = jnp.float32
    flat = mid.reshape(total, width)
    w_inner = jnp.concatenate([weights[0], weights[1], weights[2]], axis=1)
    flat = jnp.dot(flat, order, preferred_element_type=f32).astype(jnp.bfloat16)
    proj = jnp.dot(flat, w_inner, preferred_element_type=f32)
    query = proj[:, :width].reshape(frames, count, heads, depth)
    keyed = proj[:, width : 2 * width].reshape(frames, count, heads, depth)
    value = proj[:, 2 * width :].astype(jnp.bfloat16).reshape(frames, count, heads, depth)
    q_hat, q_rstd = layer_stats(query)
    k_hat, k_rstd = layer_stats(keyed)
    q_norm = q_hat * query_gain
    k_norm = k_hat * key_gain
    root = math.sqrt(depth)
    raw = jnp.einsum("fnhd,gnhd->nhfg", q_norm, k_norm, precision=high) / root
    scale = logit_scale[None, :, None, None]
    expo = jnp.exp(raw * scale)
    probs = expo / jnp.sum(expo, axis=-1, keepdims=True)
    probs_b = probs.astype(jnp.bfloat16)
    mixed = jnp.einsum("nhfg,gnhd->fnhd", probs_b, value, preferred_element_type=f32)
    mixed = mixed.astype(jnp.bfloat16).reshape(total, width)
    cot_flat = cot.reshape(total, width)
    w_out = weights[3]
    d_mixed = lax.dot_general(cot_flat, w_out, (((1,), (1,)), ((), ())), preferred_element_type=f32)
    back = (((1,), (1,)), ((), ()))
    d_mixed = lax.dot_general(d_mixed.astype(jnp.bfloat16), order, back, preferred_element_type=f32)
    d_mixed = d_mixed.astype(jnp.bfloat16).reshape(frames, count, heads, depth)
    d_probs = jnp.einsum("fnhd,gnhd->nhfg", d_mixed, value, preferred_element_type=f32)
    d_value = jnp.einsum("nhfg,fnhd->gnhd", probs_b, d_mixed, preferred_element_type=f32)
    d_value = d_value.astype(jnp.bfloat16)
    d_logits = probs * (d_probs - jnp.sum(probs * d_probs, axis=-1, keepdims=True))
    scale_term = jnp.sum(d_logits * raw, axis=(0, 2, 3))
    d_raw = d_logits * scale / root
    d_qn = jnp.einsum("nhfg,gnhd->fnhd", d_raw, k_norm, precision=high)
    d_kn = jnp.einsum("nhfg,fnhd->gnhd", d_raw, q_norm, precision=high)
    qgain_term = jnp.sum(d_qn * q_hat, axis=(0, 1, 2))
    kgain_term = jnp.sum(d_kn * k_hat, axis=(0, 1, 2))
    d_query = layer_back(d_qn * query_gain, q_hat, q_rstd).astype(jnp.bfloat16)
    d_key = layer_back(d_kn * key_gain, k_hat, k_rstd).astype(jnp.bfloat16)
    d_cat = jnp.concatenate(
        [d_query.reshape(total, width), d_key.reshape(total, width), d_value.reshape(total, width)],
        axis=1,
    )
    d_mid = lax.dot_general(d_cat, w_inner, (((1,), (1,)), ((), ())), preferred_element_type=f32)
    d_mid = lax.dot_general(d_mid.astype(jnp.bfloat16), order, back, preferred_element_type=f32)
    d_mid = d_mid.astype(jnp.bfloat16).reshape(frames, count, width)
    return (d_mid, mixed, d_value.reshape(total, width), scale_term, qgain_term, kgain_term)


def local(
    clip_input, cotangent, norm_gain, conv_weight, attn_weight, query_gain, key_gain, logit_scale
):
    source = clip_input[0]
    cot = cotangent[0]
    frames_here, rows, cols, width = source.shape
    positions = rows * cols
    per_group = width // GROUPS
    cot_flat = cot.reshape(frames_here, positions, width)
    shard = jnp.concatenate(
        [
            conv_weight.reshape(90, width),
            jnp.transpose(attn_weight.reshape(10, 4, width), (1, 0, 2)).reshape(40, width),
        ],
        axis=0,
    )
    block = column(shard).reshape(8, 13, 10, width).transpose(1, 0, 2, 3).reshape(13, 80, width)
    full_conv, attn_full = widened(block[:9], block[9:])
    order = reorder(width)
    tile = lax.axis_index("tile")
    swap = [(0, 1), (1, 0)]
    edge = jnp.where(tile == 0, source[:, rows - 1 :], source[:, :1])
    other_edge = lax.ppermute(edge, "tile", swap)
    xf = source.astype(jnp.float32).reshape(frames_here, positions, GROUPS, per_group)
    part = jnp.concatenate([jnp.sum(xf, axis=(1, 3)), jnp.sum(xf * xf, axis=(1, 3))], axis=1)
    part = part + lax.ppermute(part, "tile", swap)
    sums, squares = (part[:, :GROUPS], part[:, GROUPS:])
    count = positions * lax.axis_size("tile") * per_group
    mean = sums / count
    rstd = lax.rsqrt(squares / count - mean * mean + 1e-05)
    mean_wide = jnp.repeat(mean, per_group, axis=1)[:, None, None, :]
    rstd_wide = jnp.repeat(rstd, per_group, axis=1)[:, None, None, :]

    def activated(v):
        normed = (v.astype(jnp.float32) - mean_wide) * rstd_wide
        return jax.nn.silu(normed * norm_gain).astype(jnp.bfloat16)

    act = activated(source)
    halo = activated(other_edge)
    none = jnp.zeros_like(halo)
    before = jnp.where(tile == 1, halo, none)
    after = jnp.where(tile == 0, halo, none)
    padded = jnp.concatenate([before, act, after], axis=1)
    padded = jnp.dot(padded, order, preferred_element_type=jnp.float32).astype(jnp.bfloat16)
    padded = jnp.pad(padded, ((0, 0), (0, 0), (1, 1), (0, 0)))
    slabs = []
    for row_off in (-1, 0, 1):
        for col_off in (-1, 0, 1):
            slabs.append(
                padded[:, 1 + row_off : 1 + row_off + rows, 1 + col_off : 1 + col_off + cols, :]
            )
    stacked = jnp.stack(slabs, axis=3).reshape(frames_here * positions, 9, width)
    pre = jnp.dot(
        stacked.reshape(frames_here * positions, 9 * width),
        full_conv.reshape(9 * width, width),
        preferred_element_type=jnp.float32,
    )
    mid = (source.astype(jnp.float32) + pre.reshape(frames_here, rows, cols, width)).astype(
        jnp.bfloat16
    )
    mid_flat = mid.reshape(frames_here, positions, width)
    mid_tiled, cot_tiled = (
        lax.all_to_all(mid_flat, "frame", split_axis=1, concat_axis=0, tiled=True),
        lax.all_to_all(cot_flat, "frame", split_axis=1, concat_axis=0, tiled=True),
    )
    d_mid, mixed, d_value, scale_term, qgain_term, kgain_term = attention_pass(
        mid_tiled, cot_tiled, attn_full, order, query_gain, key_gain, logit_scale
    )
    d_back = lax.all_to_all(d_mid, "frame", split_axis=0, concat_axis=1, tiled=True)
    mid_grad = (
        cot.astype(jnp.float32) + d_back.reshape(frames_here, rows, cols, width).astype(jnp.float32)
    ).astype(jnp.bfloat16)
    tiled_mid = mid_tiled.reshape(-1, width)
    tiled_cot = cot_tiled.reshape(-1, width)
    contract = (((0,), (0,)), ((), ()))
    value_term = lax.dot_general(tiled_mid, d_value, contract, preferred_element_type=jnp.float32)
    out_term = lax.dot_general(mixed, tiled_cot, contract, preferred_element_type=jnp.float32)
    small = jnp.concatenate([scale_term, qgain_term, kgain_term])
    small = small + lax.ppermute(small, "tile", swap)
    heads, depth = (logit_scale.shape[0], query_gain.shape[0])
    length = small.shape[0]
    out_block = over_frames(paired(out_term))
    row = jnp.broadcast_to(two_parts(small, width), (32, 1, width))
    value_block = over_frames(jnp.concatenate([paired(value_term), row], axis=1))
    row = two_parts(one_part(value_block[10], length), 2 * width)
    block = jnp.concatenate([value_block[:10], out_block], axis=1).astype(jnp.bfloat16)
    block = jnp.pad(jnp.concatenate([block, row], axis=0), ((0, 5), (0, 0)))
    total = over_clips(block)
    summed = total[:10]
    small = one_part(total[10], length)
    scale_sum = small[:heads]
    qgain_sum = small[heads : heads + depth]
    kgain_sum = small[heads + depth :]
    tokens_all = lax.axis_size("dp") * mid_tiled.shape[0] * rows * lax.axis_size("tile") * cols
    factor = 1.0 / math.sqrt(tokens_all)
    value_grad = summed[:, :width] * factor
    out_proj_grad = summed[:, width:] * factor
    return (
        mid_grad[None],
        value_grad,
        out_proj_grad,
        qgain_sum * factor,
        kgain_sum * factor,
        scale_sum * factor,
    )


def solution(mesh):
    in_specs = (
        P("dp", "frame", "tile", None, None),
        P("dp", "frame", "tile", None, None),
        P(),
        P(None, ("frame", "tile"), None),
        P(("frame", "tile"), None),
        P(),
        P(),
        P(),
    )
    out_specs = (
        P("dp", "frame", "tile", None, None),
        P(("frame", "tile"), None),
        P(("frame", "tile"), None),
        P(),
        P(),
        P(),
    )
    return jax.shard_map(local, mesh=mesh, in_specs=in_specs, out_specs=out_specs, check_vma=False)
```

```python
import math

import jax
import jax.numpy as jnp
from jax import lax
from jax.experimental import pallas as pl
from jax.experimental.pallas import tpu as pltpu
from jax.sharding import PartitionSpec as P

GROUPS = 32
CORES = [(i, i + 1 - 2 * (i % 2)) for i in range(32)]


MESH = pl.DeviceIdType.MESH


def spot():
    frame, yl = (lax.axis_index("frame"), lax.axis_index("tile"))
    return ((frame // 8) * 2 + yl, (frame // 2) % 4, frame % 2)


def named(y, x, core):
    return {"frame": (y // 2) * 8 + x * 2 + core, "tile": y % 2}


def greet(peers):
    barrier = pltpu.get_barrier_semaphore()
    for peer in peers:
        pl.semaphore_signal(barrier, inc=1, device_id=peer, device_id_type=MESH)
    pl.semaphore_wait(barrier, len(peers))


def column_kernel(w_ref, out_ref, send_sem, recv_sem, own_sem):
    y, x, core = spot()
    up, down = (named((y + 1) % 8, x, core), named((y + 7) % 8, x, core))
    greet((up, down))
    sent = []

    def remote(at, to, number, own=False):
        return pltpu.make_async_remote_copy(
            src_ref=w_ref if own else out_ref.at[at],
            dst_ref=out_ref.at[at],
            send_sem=send_sem.at[number],
            recv_sem=recv_sem.at[at],
            device_id=to,
            device_id_type=MESH,
        )

    def send(dy, to, own=False):
        copy = remote((y + dy + 8) % 8, to, len(sent), own)
        copy.start()
        sent.append(copy)

    def arrived(dy):
        remote((y + dy + 8) % 8, up, 0).wait_recv()

    send(0, up, True)
    send(0, down, True)
    mine = pltpu.make_async_copy(w_ref, out_ref.at[y], own_sem)
    mine.start()
    for step in (1, 2, 3):
        arrived(-step)
        send(-step, up)
        arrived(step)
        if step < 3:
            send(step, down)
    arrived(-4)
    mine.wait()
    for copy in sent:
        copy.wait_send()


def wide_kernel(conv_in, attn_in, conv_out, attn_out, send_sem, recv_sem, whole_sem, own_sem):
    y, x, core = spot()
    z = lax.axis_index("dp")
    parity = z % 2
    ahead, behind = ({"dp": (z + 1) % 8}, {"dp": (z + 7) % 8})
    right, left = (named(y, (x + 1) % 4, core), named(y, (x + 3) % 4, core))
    twin = named(y, x, 1 - core)
    greet((ahead, behind, right, left, twin))
    sent = []

    def rows(dx, dc=0):
        number = ((x + dx + 4) % 4) * 2 + (core + dc) % 2
        return (number, pl.ds(pl.multiple_of(number * 80, 16), 80))

    def parts(unit):
        attn, at = unit
        if attn:
            return (attn_in, attn_out, at, 9 + at)
        return (conv_in, conv_out, at, at)

    def remote(unit, dx, dc, to, number, own=False):
        source, target, at, sem = parts(unit)
        block, span = rows(dx, dc)
        there = target.at[at, span]
        return pltpu.make_async_remote_copy(
            src_ref=source.at[at] if own else there,
            dst_ref=there,
            send_sem=send_sem.at[number],
            recv_sem=recv_sem.at[sem, block],
            device_id=to,
            device_id_type=MESH,
        )

    def send(unit, dx, to, own=False):
        copy = remote(unit, dx, 0, to, len(sent), own)
        copy.start()
        sent.append(copy)

    def arrived(unit, dx, dc=0):
        remote(unit, dx, dc, twin, 0).wait_recv()

    near = [(False, 2 * j + parity) for j in range(4)] + [(True, 2 * j + parity) for j in range(2)]
    far = [(False, 2 * j + 1 - parity) for j in range(4)]
    far = far + [(True, 2 * j + 1 - parity) for j in range(2)]
    near = near + [(False, 8)]
    for unit in near:
        send(unit, 0, right, True)
        send(unit, 0, left, True)
    span = rows(0)[1]
    pairs = ((conv_in, conv_out, 0), (attn_in, attn_out, 1))
    wholes = []
    for source, target, k in pairs:
        copy = pltpu.make_async_remote_copy(
            src_ref=source,
            dst_ref=target.at[:, span],
            send_sem=whole_sem.at[k],
            recv_sem=whole_sem.at[2 + k],
            device_id=twin,
            device_id_type=MESH,
        )
        copy.start()
        wholes.append(copy)
    locals_ = []
    for source, target, k in pairs:
        copy = pltpu.make_async_copy(source, target.at[:, span], own_sem.at[k])
        copy.start()
        locals_.append(copy)

    def onward(k, dx):
        if k < 6:
            send(near[k], dx, ahead if k % 2 == 0 else behind)
        send(near[k], dx, twin)

    def across(k, dx):
        arrived(far[k], dx)
        send(far[k], dx, twin)

    for k, unit in enumerate(near):
        arrived(unit, -1)
        if k % 2 == 0:
            send(unit, -1, right)
        onward(k, -1)
        arrived(unit, 1)
        if k % 2 == 1:
            send(unit, 1, left)
        onward(k, 1)
        if k >= 1:
            across(k - 1, -1)
            across(k - 1, 1)
    for k, unit in enumerate(near):
        arrived(unit, 2)
        onward(k, 2)
        if k >= 1:
            across(k - 1, 2)
    for copy in wholes:
        copy.wait_recv()
    for unit in near + far:
        for dx in (-1, 1, 2):
            arrived(unit, dx, 1)
    for copy in locals_:
        copy.wait()
    for copy in wholes + sent:
        copy.wait_send()


def column(shard):
    return pl.pallas_call(
        column_kernel,
        out_shape=jax.ShapeDtypeStruct((8,) + shard.shape, shard.dtype),
        in_specs=[pl.BlockSpec(memory_space=pltpu.VMEM)],
        out_specs=pl.BlockSpec(memory_space=pl.ANY),
        scratch_shapes=[
            pltpu.SemaphoreType.DMA((7,)),
            pltpu.SemaphoreType.DMA((8,)),
            pltpu.SemaphoreType.DMA,
        ],
        compiler_params=pltpu.CompilerParams(collective_id=0, has_side_effects=True),
    )(shard)


def widened(conv, attn):
    width = conv.shape[2]
    return pl.pallas_call(
        wide_kernel,
        out_shape=(
            jax.ShapeDtypeStruct((9, width, width), conv.dtype),
            jax.ShapeDtypeStruct((4, width, width), attn.dtype),
        ),
        in_specs=[pl.BlockSpec(memory_space=pltpu.VMEM)] * 2,
        out_specs=(pl.BlockSpec(memory_space=pl.ANY),) * 2,
        scratch_shapes=[
            pltpu.SemaphoreType.DMA((78,)),
            pltpu.SemaphoreType.DMA((13, 8)),
            pltpu.SemaphoreType.DMA((4,)),
            pltpu.SemaphoreType.DMA((2,)),
        ],
        compiler_params=pltpu.CompilerParams(collective_id=1, has_side_effects=True),
    )(conv, attn)


def clips_kernel(in_ref, out_ref, held, send_sem, recv_sem, own_sem):
    z = lax.axis_index("dp")
    greet([{"dp": (z + d) % 8} for d in range(1, 8)])
    mine = pltpu.make_async_copy(in_ref, held.at[z], own_sem)
    mine.start()
    copies = []
    for d in (4, 3, 5, 2, 6, 1, 7):
        copy = pltpu.make_async_remote_copy(
            src_ref=in_ref,
            dst_ref=held.at[z],
            send_sem=send_sem.at[d],
            recv_sem=recv_sem.at[z],
            device_id={"dp": (z + d) % 8},
            device_id_type=MESH,
        )
        copy.start()
        copies.append(copy)
    for d in range(1, 8):
        peer = (z + d) % 8
        pltpu.make_async_remote_copy(
            src_ref=in_ref,
            dst_ref=held.at[peer],
            send_sem=send_sem.at[0],
            recv_sem=recv_sem.at[peer],
            device_id={"dp": peer},
            device_id_type=MESH,
        ).wait_recv()
    mine.wait()
    total = held[0].astype(jnp.float32)
    for k in range(1, 8):
        total = total + held[k].astype(jnp.float32)
    out_ref[...] = total
    for copy in copies:
        copy.wait_send()


def over_clips(block):
    return pl.pallas_call(
        clips_kernel,
        out_shape=jax.ShapeDtypeStruct(block.shape, jnp.float32),
        in_specs=[pl.BlockSpec(memory_space=pltpu.VMEM)],
        out_specs=pl.BlockSpec(memory_space=pltpu.VMEM),
        scratch_shapes=[
            pltpu.VMEM((8,) + block.shape, block.dtype),
            pltpu.SemaphoreType.DMA((8,)),
            pltpu.SemaphoreType.DMA((8,)),
            pltpu.SemaphoreType.DMA,
        ],
        compiler_params=pltpu.CompilerParams(collective_id=2, has_side_effects=True),
    )(block)


def reorder(width):
    place = lax.broadcasted_iota(jnp.int32, (width, width), 1)
    origin = ((place // 20) % 4) * 160 + (place // 80) * 20 + place % 20
    return (lax.broadcasted_iota(jnp.int32, (width, width), 0) == origin).astype(jnp.bfloat16)


def paired(terms):
    width = terms.shape[1]
    core = lax.axis_index("frame") % 2
    halves = terms.reshape(16, 2, 20, width)
    mine = lax.dynamic_index_in_dim(halves, core, 1, keepdims=False)
    theirs = lax.dynamic_index_in_dim(halves, 1 - core, 1, keepdims=False).astype(jnp.bfloat16)
    got = lax.ppermute(theirs, "frame", CORES)
    return (mine + got.astype(jnp.float32)).astype(jnp.bfloat16)


def over_chips(blocks, small):
    width = blocks.shape[2]
    row = jnp.broadcast_to(two_parts(small, width), (16, 1, width))
    groups = [list(range(core, 32, 2)) for core in (0, 1)]
    got = lax.all_to_all(
        jnp.concatenate([blocks, row], axis=1),
        "frame",
        split_axis=0,
        concat_axis=0,
        tiled=True,
        axis_index_groups=groups,
    )
    return jnp.sum(got.astype(jnp.float32), axis=0)


def over_tiles(total, length):
    width = total.shape[1]
    tile = lax.axis_index("tile")
    halves = total[:20].reshape(2, 10, width)
    mine = lax.dynamic_index_in_dim(halves, tile, 0, keepdims=False)
    theirs = lax.dynamic_index_in_dim(halves, 1 - tile, 0, keepdims=False)
    row = two_parts(one_part(total[20], length), width)
    theirs = jnp.concatenate([theirs.astype(jnp.bfloat16), row], axis=0)
    other = lax.ppermute(theirs, "tile", [(0, 1), (1, 0)]).astype(jnp.float32)
    own_row = one_part(row[0].astype(jnp.float32), length)
    return (mine + other[:10], own_row + one_part(other[10], length))


def two_parts(small, width):
    high = lax.reduce_precision(small, 8, 7)
    row = jnp.concatenate([high, small - high]).astype(jnp.bfloat16)
    return jnp.pad(row, (0, width - row.shape[0]))[None]


def one_part(row, length):
    return row[:length] + row[length : 2 * length]


def layer_stats(vec):
    mean = jnp.mean(vec, axis=-1, keepdims=True)
    cent = vec - mean
    var = jnp.mean(cent * cent, axis=-1, keepdims=True)
    rstd = lax.rsqrt(var + 1e-05)
    return (cent * rstd, rstd)


def layer_back(dhat, hat, rstd):
    first = jnp.mean(dhat, axis=-1, keepdims=True)
    second = jnp.mean(dhat * hat, axis=-1, keepdims=True)
    return rstd * (dhat - first - hat * second)


def attention_pass(mid, cot, weights, order, query_gain, key_gain, logit_scale):
    frames, count, width = mid.shape
    heads = logit_scale.shape[0]
    depth = width // heads
    total = frames * count
    high = lax.Precision.HIGHEST
    f32 = jnp.float32
    flat = mid.reshape(total, width)
    w_inner = jnp.concatenate([weights[0], weights[1], weights[2]], axis=1)
    flat = jnp.dot(flat, order, preferred_element_type=f32).astype(jnp.bfloat16)
    proj = jnp.dot(flat, w_inner, preferred_element_type=f32)
    query = proj[:, :width].reshape(frames, count, heads, depth)
    keyed = proj[:, width : 2 * width].reshape(frames, count, heads, depth)
    value = proj[:, 2 * width :].astype(jnp.bfloat16).reshape(frames, count, heads, depth)
    q_hat, q_rstd = layer_stats(query)
    k_hat, k_rstd = layer_stats(keyed)
    q_norm = q_hat * query_gain
    k_norm = k_hat * key_gain
    root = math.sqrt(depth)
    raw = jnp.einsum("fnhd,gnhd->nhfg", q_norm, k_norm, precision=high) / root
    scale = logit_scale[None, :, None, None]
    expo = jnp.exp(raw * scale)
    probs = expo / jnp.sum(expo, axis=-1, keepdims=True)
    probs_b = probs.astype(jnp.bfloat16)
    mixed = jnp.einsum("nhfg,gnhd->fnhd", probs_b, value, preferred_element_type=f32)
    mixed = mixed.astype(jnp.bfloat16).reshape(total, width)
    cot_flat = cot.reshape(total, width)
    w_out = weights[3]
    d_mixed = lax.dot_general(cot_flat, w_out, (((1,), (1,)), ((), ())), preferred_element_type=f32)
    back = (((1,), (1,)), ((), ()))
    d_mixed = lax.dot_general(d_mixed.astype(jnp.bfloat16), order, back, preferred_element_type=f32)
    d_mixed = d_mixed.astype(jnp.bfloat16).reshape(frames, count, heads, depth)
    d_probs = jnp.einsum("fnhd,gnhd->nhfg", d_mixed, value, preferred_element_type=f32)
    d_value = jnp.einsum("nhfg,fnhd->gnhd", probs_b, d_mixed, preferred_element_type=f32)
    d_value = d_value.astype(jnp.bfloat16)
    d_logits = probs * (d_probs - jnp.sum(probs * d_probs, axis=-1, keepdims=True))
    contract = (((0,), (0,)), ((), ()))
    d_value = d_value.reshape(total, width)
    value_term = lax.dot_general(
        mid.reshape(total, width), d_value, contract, preferred_element_type=f32
    )
    out_term = lax.dot_general(mixed, cot_flat, contract, preferred_element_type=f32)
    terms = jnp.concatenate([value_term, out_term], axis=1)
    d_logits, terms = lax.optimization_barrier((d_logits, terms))
    pair = paired(terms)
    scale_term = jnp.sum(d_logits * raw, axis=(0, 2, 3))
    d_raw = d_logits * scale / root
    d_qn = jnp.einsum("nhfg,gnhd->fnhd", d_raw, k_norm, precision=high)
    d_kn = jnp.einsum("nhfg,fnhd->gnhd", d_raw, q_norm, precision=high)
    d_qn, d_kn, pair = lax.optimization_barrier((d_qn, d_kn, pair))
    qgain_term = jnp.sum(d_qn * q_hat, axis=(0, 1, 2))
    kgain_term = jnp.sum(d_kn * k_hat, axis=(0, 1, 2))
    d_query = layer_back(d_qn * query_gain, q_hat, q_rstd).astype(jnp.bfloat16)
    d_key = layer_back(d_kn * key_gain, k_hat, k_rstd).astype(jnp.bfloat16)
    d_cat = jnp.concatenate(
        [d_query.reshape(total, width), d_key.reshape(total, width), d_value.reshape(total, width)],
        axis=1,
    )
    small = jnp.concatenate([scale_term, qgain_term, kgain_term])
    small = small + lax.ppermute(small, "frame", CORES)
    total_plane = over_chips(pair, small)
    d_mid = lax.dot_general(d_cat, w_inner, (((1,), (1,)), ((), ())), preferred_element_type=f32)
    d_mid = lax.dot_general(d_mid.astype(jnp.bfloat16), order, back, preferred_element_type=f32)
    d_mid = d_mid.astype(jnp.bfloat16).reshape(frames, count, width)
    d_mid, total_plane = lax.optimization_barrier((d_mid, total_plane))
    sums, small = over_tiles(total_plane, small.shape[0])
    return (d_mid, sums, small)


def local(
    clip_input, cotangent, norm_gain, conv_weight, attn_weight, query_gain, key_gain, logit_scale
):
    source = clip_input[0]
    cot = cotangent[0]
    frames_here, rows, cols, width = source.shape
    positions = rows * cols
    per_group = width // GROUPS
    cot_flat = cot.reshape(frames_here, positions, width)
    shard = jnp.concatenate(
        [
            conv_weight.reshape(90, width),
            jnp.transpose(attn_weight.reshape(10, 4, width), (1, 0, 2)).reshape(40, width),
        ],
        axis=0,
    )
    block = column(shard).reshape(8, 13, 10, width).transpose(1, 0, 2, 3).reshape(13, 80, width)
    full_conv, attn_full = widened(block[:9], block[9:])
    order = reorder(width)
    tile = lax.axis_index("tile")
    swap = [(0, 1), (1, 0)]
    edge = jnp.where(tile == 0, source[:, rows - 1 :], source[:, :1])
    other_edge = lax.ppermute(edge, "tile", swap)
    xf = source.astype(jnp.float32).reshape(frames_here, positions, GROUPS, per_group)
    part = jnp.concatenate([jnp.sum(xf, axis=(1, 3)), jnp.sum(xf * xf, axis=(1, 3))], axis=1)
    part = part + lax.ppermute(part, "tile", swap)
    sums, squares = (part[:, :GROUPS], part[:, GROUPS:])
    count = positions * lax.axis_size("tile") * per_group
    mean = sums / count
    rstd = lax.rsqrt(squares / count - mean * mean + 1e-05)
    mean_wide = jnp.repeat(mean, per_group, axis=1)[:, None, None, :]
    rstd_wide = jnp.repeat(rstd, per_group, axis=1)[:, None, None, :]

    def activated(v):
        normed = (v.astype(jnp.float32) - mean_wide) * rstd_wide
        return jax.nn.silu(normed * norm_gain).astype(jnp.bfloat16)

    act = activated(source)
    halo = activated(other_edge)
    none = jnp.zeros_like(halo)
    before = jnp.where(tile == 1, halo, none)
    after = jnp.where(tile == 0, halo, none)
    padded = jnp.concatenate([before, act, after], axis=1)
    padded = jnp.dot(padded, order, preferred_element_type=jnp.float32).astype(jnp.bfloat16)
    padded = jnp.pad(padded, ((0, 0), (0, 0), (1, 1), (0, 0)))
    slabs = []
    for row_off in (-1, 0, 1):
        for col_off in (-1, 0, 1):
            slabs.append(
                padded[:, 1 + row_off : 1 + row_off + rows, 1 + col_off : 1 + col_off + cols, :]
            )
    stacked = jnp.stack(slabs, axis=3).reshape(frames_here * positions, 9, width)
    pre = jnp.dot(
        stacked.reshape(frames_here * positions, 9 * width),
        full_conv.reshape(9 * width, width),
        preferred_element_type=jnp.float32,
    )
    mid = (source.astype(jnp.float32) + pre.reshape(frames_here, rows, cols, width)).astype(
        jnp.bfloat16
    )
    mid_flat = mid.reshape(frames_here, positions, width)
    mid_tiled, cot_tiled = (
        lax.all_to_all(mid_flat, "frame", split_axis=1, concat_axis=0, tiled=True),
        lax.all_to_all(cot_flat, "frame", split_axis=1, concat_axis=0, tiled=True),
    )
    d_mid, sums, small = attention_pass(
        mid_tiled, cot_tiled, attn_full, order, query_gain, key_gain, logit_scale
    )
    d_back = lax.all_to_all(d_mid, "frame", split_axis=0, concat_axis=1, tiled=True)
    mid_grad = (
        cot.astype(jnp.float32) + d_back.reshape(frames_here, rows, cols, width).astype(jnp.float32)
    ).astype(jnp.bfloat16)
    heads, depth = (logit_scale.shape[0], query_gain.shape[0])
    length = small.shape[0]
    row = two_parts(small, 2 * width)
    block = sums.astype(jnp.bfloat16)
    block = jnp.pad(jnp.concatenate([block, row], axis=0), ((0, 5), (0, 0)))
    total = over_clips(block)
    summed = total[:10]
    small = one_part(total[10], length)
    scale_sum = small[:heads]
    qgain_sum = small[heads : heads + depth]
    kgain_sum = small[heads + depth :]
    tokens_all = lax.axis_size("dp") * mid_tiled.shape[0] * rows * lax.axis_size("tile") * cols
    factor = 1.0 / math.sqrt(tokens_all)
    value_grad = summed[:, :width] * factor
    out_proj_grad = summed[:, width:] * factor
    return (
        mid_grad[None],
        value_grad,
        out_proj_grad,
        qgain_sum * factor,
        kgain_sum * factor,
        scale_sum * factor,
    )


def solution(mesh):
    in_specs = (
        P("dp", "frame", "tile", None, None),
        P("dp", "frame", "tile", None, None),
        P(),
        P(None, ("frame", "tile"), None),
        P(("frame", "tile"), None),
        P(),
        P(),
        P(),
    )
    out_specs = (
        P("dp", "frame", "tile", None, None),
        P(("frame", "tile"), None),
        P(("frame", "tile"), None),
        P(),
        P(),
        P(),
    )
    return jax.shard_map(local, mesh=mesh, in_specs=in_specs, out_specs=out_specs, check_vma=False)
```

```python
import math

import jax
import jax.numpy as jnp
from jax import lax
from jax.experimental import pallas as pl
from jax.experimental.pallas import tpu as pltpu
from jax.sharding import PartitionSpec as P

GROUPS = 32
CORES = [(i, i + 1 - 2 * (i % 2)) for i in range(32)]


MESH = pl.DeviceIdType.MESH


def spot():
    frame, yl = (lax.axis_index("frame"), lax.axis_index("tile"))
    return ((frame // 8) * 2 + yl, (frame // 2) % 4, frame % 2)


def named(y, x, core):
    return {"frame": (y // 2) * 8 + x * 2 + core, "tile": y % 2}


def greet(peers):
    barrier = pltpu.get_barrier_semaphore()
    for peer in peers:
        pl.semaphore_signal(barrier, inc=1, device_id=peer, device_id_type=MESH)
    pl.semaphore_wait(barrier, len(peers))


def column_kernel(w_ref, out_ref, send_sem, recv_sem, own_sem):
    y, x, core = spot()
    up, down = (named((y + 1) % 8, x, core), named((y + 7) % 8, x, core))
    greet((up, down))
    sent = []

    def remote(at, to, number, own=False):
        return pltpu.make_async_remote_copy(
            src_ref=w_ref if own else out_ref.at[at],
            dst_ref=out_ref.at[at],
            send_sem=send_sem.at[number],
            recv_sem=recv_sem.at[at],
            device_id=to,
            device_id_type=MESH,
        )

    def send(dy, to, own=False):
        copy = remote((y + dy + 8) % 8, to, len(sent), own)
        copy.start()
        sent.append(copy)

    def arrived(dy):
        remote((y + dy + 8) % 8, up, 0).wait_recv()

    send(0, up, True)
    send(0, down, True)
    mine = pltpu.make_async_copy(w_ref, out_ref.at[y], own_sem)
    mine.start()
    for step in (1, 2, 3):
        arrived(-step)
        send(-step, up)
        arrived(step)
        if step < 3:
            send(step, down)
    arrived(-4)
    mine.wait()
    for copy in sent:
        copy.wait_send()


def wide_kernel(conv_in, attn_in, conv_out, attn_out, send_sem, recv_sem, whole_sem, own_sem):
    y, x, core = spot()
    z = lax.axis_index("dp")
    parity = z % 2
    ahead, behind = ({"dp": (z + 1) % 8}, {"dp": (z + 7) % 8})
    right, left = (named(y, (x + 1) % 4, core), named(y, (x + 3) % 4, core))
    twin = named(y, x, 1 - core)
    greet((ahead, behind, right, left, twin))
    sent = []

    def rows(dx, dc=0):
        number = ((x + dx + 4) % 4) * 2 + (core + dc) % 2
        return (number, pl.ds(pl.multiple_of(number * 80, 16), 80))

    def parts(unit):
        attn, at = unit
        if attn:
            return (attn_in, attn_out, at, 9 + at)
        return (conv_in, conv_out, at, at)

    def remote(unit, dx, dc, to, number, own=False):
        source, target, at, sem = parts(unit)
        block, span = rows(dx, dc)
        there = target.at[at, span]
        return pltpu.make_async_remote_copy(
            src_ref=source.at[at] if own else there,
            dst_ref=there,
            send_sem=send_sem.at[number],
            recv_sem=recv_sem.at[sem, block],
            device_id=to,
            device_id_type=MESH,
        )

    def send(unit, dx, to, own=False):
        copy = remote(unit, dx, 0, to, len(sent), own)
        copy.start()
        sent.append(copy)

    def arrived(unit, dx, dc=0):
        remote(unit, dx, dc, twin, 0).wait_recv()

    near = [(False, 2 * j + parity) for j in range(4)] + [(True, 2 * j + parity) for j in range(2)]
    far = [(False, 2 * j + 1 - parity) for j in range(4)]
    far = far + [(True, 2 * j + 1 - parity) for j in range(2)]
    near = near + [(False, 8)]
    for unit in near:
        send(unit, 0, right, True)
        send(unit, 0, left, True)
    span = rows(0)[1]
    pairs = ((conv_in, conv_out, 0), (attn_in, attn_out, 1))
    wholes = []
    for source, target, k in pairs:
        copy = pltpu.make_async_remote_copy(
            src_ref=source,
            dst_ref=target.at[:, span],
            send_sem=whole_sem.at[k],
            recv_sem=whole_sem.at[2 + k],
            device_id=twin,
            device_id_type=MESH,
        )
        copy.start()
        wholes.append(copy)
    locals_ = []
    for source, target, k in pairs:
        copy = pltpu.make_async_copy(source, target.at[:, span], own_sem.at[k])
        copy.start()
        locals_.append(copy)

    def onward(k, dx):
        if k < 6:
            send(near[k], dx, ahead if k % 2 == 0 else behind)
        send(near[k], dx, twin)

    def across(k, dx):
        arrived(far[k], dx)
        send(far[k], dx, twin)

    for k, unit in enumerate(near):
        arrived(unit, -1)
        if k % 2 == 0:
            send(unit, -1, right)
        onward(k, -1)
        arrived(unit, 1)
        if k % 2 == 1:
            send(unit, 1, left)
        onward(k, 1)
        if k >= 1:
            across(k - 1, -1)
            across(k - 1, 1)
    for k, unit in enumerate(near):
        arrived(unit, 2)
        onward(k, 2)
        if k >= 1:
            across(k - 1, 2)
    for copy in wholes:
        copy.wait_recv()
    for unit in near + far:
        for dx in (-1, 1, 2):
            arrived(unit, dx, 1)
    for copy in locals_:
        copy.wait()
    for copy in wholes + sent:
        copy.wait_send()


def column(shard):
    return pl.pallas_call(
        column_kernel,
        out_shape=jax.ShapeDtypeStruct((8,) + shard.shape, shard.dtype),
        in_specs=[pl.BlockSpec(memory_space=pltpu.VMEM)],
        out_specs=pl.BlockSpec(memory_space=pl.ANY),
        scratch_shapes=[
            pltpu.SemaphoreType.DMA((7,)),
            pltpu.SemaphoreType.DMA((8,)),
            pltpu.SemaphoreType.DMA,
        ],
        compiler_params=pltpu.CompilerParams(collective_id=0, has_side_effects=True),
    )(shard)


def widened(conv, attn):
    width = conv.shape[2]
    return pl.pallas_call(
        wide_kernel,
        out_shape=(
            jax.ShapeDtypeStruct((9, width, width), conv.dtype),
            jax.ShapeDtypeStruct((4, width, width), attn.dtype),
        ),
        in_specs=[pl.BlockSpec(memory_space=pltpu.VMEM)] * 2,
        out_specs=(pl.BlockSpec(memory_space=pl.ANY),) * 2,
        scratch_shapes=[
            pltpu.SemaphoreType.DMA((78,)),
            pltpu.SemaphoreType.DMA((13, 8)),
            pltpu.SemaphoreType.DMA((4,)),
            pltpu.SemaphoreType.DMA((2,)),
        ],
        compiler_params=pltpu.CompilerParams(collective_id=1, has_side_effects=True),
    )(conv, attn)


def clips_kernel(in_ref, out_ref, held, send_sem, recv_sem, own_sem):
    z = lax.axis_index("dp")
    greet([{"dp": (z + d) % 8} for d in range(1, 8)])
    mine = pltpu.make_async_copy(in_ref, held.at[z], own_sem)
    mine.start()
    copies = []
    for d in (4, 3, 5, 2, 6, 1, 7):
        copy = pltpu.make_async_remote_copy(
            src_ref=in_ref,
            dst_ref=held.at[z],
            send_sem=send_sem.at[d],
            recv_sem=recv_sem.at[z],
            device_id={"dp": (z + d) % 8},
            device_id_type=MESH,
        )
        copy.start()
        copies.append(copy)
    for d in range(1, 8):
        peer = (z + d) % 8
        pltpu.make_async_remote_copy(
            src_ref=in_ref,
            dst_ref=held.at[peer],
            send_sem=send_sem.at[0],
            recv_sem=recv_sem.at[peer],
            device_id={"dp": peer},
            device_id_type=MESH,
        ).wait_recv()
    mine.wait()
    total = held[0].astype(jnp.float32)
    for k in range(1, 8):
        total = total + held[k].astype(jnp.float32)
    out_ref[...] = total
    for copy in copies:
        copy.wait_send()


def over_clips(block):
    return pl.pallas_call(
        clips_kernel,
        out_shape=jax.ShapeDtypeStruct(block.shape, jnp.float32),
        in_specs=[pl.BlockSpec(memory_space=pltpu.VMEM)],
        out_specs=pl.BlockSpec(memory_space=pltpu.VMEM),
        scratch_shapes=[
            pltpu.VMEM((8,) + block.shape, block.dtype),
            pltpu.SemaphoreType.DMA((8,)),
            pltpu.SemaphoreType.DMA((8,)),
            pltpu.SemaphoreType.DMA,
        ],
        compiler_params=pltpu.CompilerParams(collective_id=2, has_side_effects=True),
    )(block)


def reorder(width):
    place = lax.broadcasted_iota(jnp.int32, (width, width), 1)
    origin = ((place // 20) % 4) * 160 + (place // 80) * 20 + place % 20
    return (lax.broadcasted_iota(jnp.int32, (width, width), 0) == origin).astype(jnp.bfloat16)


def paired(terms):
    width = terms.shape[1]
    core = lax.axis_index("frame") % 2
    halves = terms.reshape(16, 2, 20, width)
    mine = lax.dynamic_index_in_dim(halves, core, 1, keepdims=False)
    theirs = lax.dynamic_index_in_dim(halves, 1 - core, 1, keepdims=False)
    got = lax.ppermute(theirs, "frame", CORES)
    return (mine.astype(jnp.float32) + got.astype(jnp.float32)).astype(jnp.bfloat16)


def over_chips(blocks, small):
    width = blocks.shape[2]
    row = jnp.broadcast_to(two_parts(small, width), (16, 1, width))
    groups = [list(range(core, 32, 2)) for core in (0, 1)]
    got = lax.all_to_all(
        jnp.concatenate([blocks, row], axis=1),
        "frame",
        split_axis=0,
        concat_axis=0,
        tiled=True,
        axis_index_groups=groups,
    )
    return jnp.sum(got.astype(jnp.float32), axis=0)


def over_tiles(total, length):
    width = total.shape[1]
    tile = lax.axis_index("tile")
    halves = total[:20].reshape(2, 10, width)
    mine = lax.dynamic_index_in_dim(halves, tile, 0, keepdims=False)
    theirs = lax.dynamic_index_in_dim(halves, 1 - tile, 0, keepdims=False)
    row = two_parts(one_part(total[20], length), width)
    theirs = jnp.concatenate([theirs.astype(jnp.bfloat16), row], axis=0)
    other = lax.ppermute(theirs, "tile", [(0, 1), (1, 0)]).astype(jnp.float32)
    own_row = one_part(row[0].astype(jnp.float32), length)
    return (mine + other[:10], own_row + one_part(other[10], length))


def two_parts(small, width):
    high = lax.reduce_precision(small, 8, 7)
    row = jnp.concatenate([high, small - high]).astype(jnp.bfloat16)
    return jnp.pad(row, (0, width - row.shape[0]))[None]


def one_part(row, length):
    return row[:length] + row[length : 2 * length]


def layer_stats(vec):
    mean = jnp.mean(vec, axis=-1, keepdims=True)
    cent = vec - mean
    var = jnp.mean(cent * cent, axis=-1, keepdims=True)
    rstd = lax.rsqrt(var + 1e-05)
    return (cent * rstd, rstd)


def layer_back(dhat, hat, rstd):
    first = jnp.mean(dhat, axis=-1, keepdims=True)
    second = jnp.mean(dhat * hat, axis=-1, keepdims=True)
    return rstd * (dhat - first - hat * second)


def attention_pass(mid, cot, weights, order, query_gain, key_gain, logit_scale):
    frames, count, width = mid.shape
    heads = logit_scale.shape[0]
    depth = width // heads
    total = frames * count
    high = lax.Precision.HIGHEST
    f32 = jnp.float32
    flat = mid.reshape(total, width)
    w_inner = jnp.concatenate([weights[0], weights[1], weights[2]], axis=1)
    flat = jnp.dot(flat, order, preferred_element_type=f32).astype(jnp.bfloat16)
    proj = jnp.dot(flat, w_inner, preferred_element_type=f32)
    query = proj[:, :width].reshape(frames, count, heads, depth)
    keyed = proj[:, width : 2 * width].reshape(frames, count, heads, depth)
    value = proj[:, 2 * width :].astype(jnp.bfloat16).reshape(frames, count, heads, depth)
    q_hat, q_rstd = layer_stats(query)
    k_hat, k_rstd = layer_stats(keyed)
    q_norm = q_hat * query_gain
    k_norm = k_hat * key_gain
    root = math.sqrt(depth)
    raw = jnp.einsum("fnhd,gnhd->nhfg", q_norm, k_norm, precision=high) / root
    scale = logit_scale[None, :, None, None]
    expo = jnp.exp(raw * scale)
    probs = expo / jnp.sum(expo, axis=-1, keepdims=True)
    probs_b = probs.astype(jnp.bfloat16)
    mixed = jnp.einsum("nhfg,gnhd->fnhd", probs_b, value, preferred_element_type=f32)
    mixed = mixed.astype(jnp.bfloat16).reshape(total, width)
    cot_flat = cot.reshape(total, width)
    w_out = weights[3]
    d_mixed = lax.dot_general(cot_flat, w_out, (((1,), (1,)), ((), ())), preferred_element_type=f32)
    back = (((1,), (1,)), ((), ()))
    d_mixed = lax.dot_general(d_mixed.astype(jnp.bfloat16), order, back, preferred_element_type=f32)
    d_mixed = d_mixed.astype(jnp.bfloat16).reshape(frames, count, heads, depth)
    d_probs = jnp.einsum("fnhd,gnhd->nhfg", d_mixed, value, preferred_element_type=f32)
    d_value = jnp.einsum("nhfg,fnhd->gnhd", probs_b, d_mixed, preferred_element_type=f32)
    d_value = d_value.astype(jnp.bfloat16)
    d_logits = probs * (d_probs - jnp.sum(probs * d_probs, axis=-1, keepdims=True))
    contract = (((0,), (0,)), ((), ()))
    d_value = d_value.reshape(total, width)
    value_term = lax.dot_general(
        mid.reshape(total, width), d_value, contract, preferred_element_type=f32
    )
    out_term = lax.dot_general(mixed, cot_flat, contract, preferred_element_type=f32)
    terms = [value_term.astype(jnp.bfloat16), out_term.astype(jnp.bfloat16)]
    terms = jnp.concatenate(terms, axis=1)
    d_logits, terms = lax.optimization_barrier((d_logits, terms))
    pair = paired(terms)
    scale_term = jnp.sum(d_logits * raw, axis=(0, 2, 3))
    d_raw = d_logits * scale / root
    d_qn = jnp.einsum("nhfg,gnhd->fnhd", d_raw, k_norm, precision=high)
    d_kn = jnp.einsum("nhfg,fnhd->gnhd", d_raw, q_norm, precision=high)
    d_qn, d_kn, pair = lax.optimization_barrier((d_qn, d_kn, pair))
    qgain_term = jnp.sum(d_qn * q_hat, axis=(0, 1, 2))
    kgain_term = jnp.sum(d_kn * k_hat, axis=(0, 1, 2))
    d_query = layer_back(d_qn * query_gain, q_hat, q_rstd).astype(jnp.bfloat16)
    d_key = layer_back(d_kn * key_gain, k_hat, k_rstd).astype(jnp.bfloat16)
    d_cat = jnp.concatenate(
        [d_query.reshape(total, width), d_key.reshape(total, width), d_value.reshape(total, width)],
        axis=1,
    )
    small = jnp.concatenate([scale_term, qgain_term, kgain_term])
    small = small + lax.ppermute(small, "frame", CORES)
    total_plane = over_chips(pair, small)
    d_mid = lax.dot_general(d_cat, w_inner, (((1,), (1,)), ((), ())), preferred_element_type=f32)
    d_mid = lax.dot_general(d_mid.astype(jnp.bfloat16), order, back, preferred_element_type=f32)
    d_mid = d_mid.astype(jnp.bfloat16).reshape(frames, count, width)
    d_mid, total_plane = lax.optimization_barrier((d_mid, total_plane))
    sums, small = over_tiles(total_plane, small.shape[0])
    return (d_mid, sums, small)


def local(
    clip_input, cotangent, norm_gain, conv_weight, attn_weight, query_gain, key_gain, logit_scale
):
    source = clip_input[0]
    cot = cotangent[0]
    frames_here, rows, cols, width = source.shape
    positions = rows * cols
    per_group = width // GROUPS
    cot_flat = cot.reshape(frames_here, positions, width)
    shard = jnp.concatenate(
        [
            conv_weight.reshape(90, width),
            jnp.transpose(attn_weight.reshape(10, 4, width), (1, 0, 2)).reshape(40, width),
        ],
        axis=0,
    )
    block = column(shard).reshape(8, 13, 10, width).transpose(1, 0, 2, 3).reshape(13, 80, width)
    full_conv, attn_full = widened(block[:9], block[9:])
    order = reorder(width)
    tile = lax.axis_index("tile")
    swap = [(0, 1), (1, 0)]
    edge = jnp.where(tile == 0, source[:, rows - 1 :], source[:, :1])
    other_edge = lax.ppermute(edge, "tile", swap)
    xf = source.astype(jnp.float32).reshape(frames_here, positions, GROUPS, per_group)
    part = jnp.concatenate([jnp.sum(xf, axis=(1, 3)), jnp.sum(xf * xf, axis=(1, 3))], axis=1)
    part = part + lax.ppermute(part, "tile", swap)
    sums, squares = (part[:, :GROUPS], part[:, GROUPS:])
    count = positions * lax.axis_size("tile") * per_group
    mean = sums / count
    rstd = lax.rsqrt(squares / count - mean * mean + 1e-05)
    mean_wide = jnp.repeat(mean, per_group, axis=1)[:, None, None, :]
    rstd_wide = jnp.repeat(rstd, per_group, axis=1)[:, None, None, :]

    def activated(v):
        normed = (v.astype(jnp.float32) - mean_wide) * rstd_wide
        return jax.nn.silu(normed * norm_gain).astype(jnp.bfloat16)

    act = activated(source)
    halo = activated(other_edge)
    none = jnp.zeros_like(halo)
    before = jnp.where(tile == 1, halo, none)
    after = jnp.where(tile == 0, halo, none)
    padded = jnp.concatenate([before, act, after], axis=1)
    padded = jnp.dot(padded, order, preferred_element_type=jnp.float32).astype(jnp.bfloat16)
    padded = jnp.pad(padded, ((0, 0), (0, 0), (1, 1), (0, 0)))
    slabs = []
    for row_off in (-1, 0, 1):
        for col_off in (-1, 0, 1):
            slabs.append(
                padded[:, 1 + row_off : 1 + row_off + rows, 1 + col_off : 1 + col_off + cols, :]
            )
    stacked = jnp.stack(slabs, axis=3).reshape(frames_here * positions, 9, width)
    pre = jnp.dot(
        stacked.reshape(frames_here * positions, 9 * width),
        full_conv.reshape(9 * width, width),
        preferred_element_type=jnp.float32,
    )
    mid = (source.astype(jnp.float32) + pre.reshape(frames_here, rows, cols, width)).astype(
        jnp.bfloat16
    )
    share = positions // 32
    mid_tiled, cot_tiled = (
        lax.all_to_all(
            mid.reshape(32, share, width), "frame", split_axis=0, concat_axis=0, tiled=True
        ),
        lax.all_to_all(
            cot_flat.reshape(32, share, width), "frame", split_axis=0, concat_axis=0, tiled=True
        ),
    )
    d_mid, sums, small = attention_pass(
        mid_tiled, cot_tiled, attn_full, order, query_gain, key_gain, logit_scale
    )
    d_back = lax.all_to_all(d_mid, "frame", split_axis=0, concat_axis=0, tiled=True)
    mid_grad = (
        cot.astype(jnp.float32) + d_back.reshape(frames_here, rows, cols, width).astype(jnp.float32)
    ).astype(jnp.bfloat16)
    heads, depth = (logit_scale.shape[0], query_gain.shape[0])
    length = small.shape[0]
    row = two_parts(small, 2 * width)
    block = sums.astype(jnp.bfloat16)
    block = jnp.pad(jnp.concatenate([block, row], axis=0), ((0, 5), (0, 0)))
    total = over_clips(block)
    summed = total[:10]
    small = one_part(total[10], length)
    scale_sum = small[:heads]
    qgain_sum = small[heads : heads + depth]
    kgain_sum = small[heads + depth :]
    tokens_all = lax.axis_size("dp") * mid_tiled.shape[0] * rows * lax.axis_size("tile") * cols
    factor = 1.0 / math.sqrt(tokens_all)
    value_grad = summed[:, :width] * factor
    out_proj_grad = summed[:, width:] * factor
    return (
        mid_grad[None],
        value_grad,
        out_proj_grad,
        qgain_sum * factor,
        kgain_sum * factor,
        scale_sum * factor,
    )


def solution(mesh):
    in_specs = (
        P("dp", "frame", "tile", None, None),
        P("dp", "frame", "tile", None, None),
        P(),
        P(None, ("frame", "tile"), None),
        P(("frame", "tile"), None),
        P(),
        P(),
        P(),
    )
    out_specs = (
        P("dp", "frame", "tile", None, None),
        P(("frame", "tile"), None),
        P(("frame", "tile"), None),
        P(),
        P(),
        P(),
    )
    return jax.shard_map(local, mesh=mesh, in_specs=in_specs, out_specs=out_specs, check_vma=False)
```
